32 devices in a mesh: ctx: 16 (over z, x, core), chan: 2 (over y).
Axes of the slice: x: 2, y: 2, z: 4, core: 2. Of those that a mesh axis runs over, the one named last changes fastest.
Arguments:
- query_act: bfloat16 [2048, 1024], P('ctx', 'chan'), may hold values from -6 to 6
- key_act: bfloat16 [2048, 1024], P('ctx', 'chan'), may hold values from -6 to 6
- value_act: bfloat16 [2048, 1024], P('ctx', 'chan'), may hold values from -6 to 6
- filters: bfloat16 [2048, 1024], P('ctx', 'chan'), may hold values from -0.125 to 0.125
- skip_scale: float32 [1024], P('chan'), may hold values from -4 to 4
- w_out: bfloat16 [1024, 4096], P('chan'), may hold values from -0.25 to 0.25
Outputs:
- projected: bfloat16 [2048, 4096], P('ctx', 'chan')
The draws below stay inside these ranges and needn't reach their ends.
All inputs are finite; a program needn't handle non-finite values.
Results may differ from the reference program's by a relative error of at most 0.015.
Values may be sent and summed in bfloat16 or wider, within the bound.
A program may use at most 64 MiB of HBM per device.

```python
import jax
import jax.numpy as jnp
from jax import lax

D = 4096
CH_DEV = 512
SEQ = 2048
CHANNELS = 1024
N_CHAN = 2


def strengthened(values, rng, source, target, blocks, factor):
    def block_of(position):
        return (jnp.arange(values.shape[position]) // (values.shape[position] // blocks)).reshape((-1,) + (1,) * (values.ndim - 1 - position))

    one_side = jax.random.permutation(rng, blocks)[block_of(target)]
    far = (block_of(target) + blocks // 2) % blocks
    return jnp.where((block_of(source) == one_side) | (block_of(source) == far), factor * values, values)


def level_of(rng, dims, shards, low, largest):
    gain, own = 1.0, jax.random.fold_in(rng, 6)
    for position, shards_of in shards:
        draws = jnp.exp(jax.random.uniform(jax.random.fold_in(own, position), (shards_of,), jnp.float32, low / len(shards), largest / len(shards)))
        gain = gain * jnp.repeat(draws, dims[position] // shards_of).reshape([-1 if axis == position else 1 for axis in range(len(dims))])
    return gain


def bell_draw(own_key, extent, deviation, bound, pieces=(), kind=jnp.bfloat16):
    drawn = jax.random.normal(own_key, extent, jnp.float32) * deviation
    if len(pieces) > 0:
        drawn = level_of(own_key, extent, pieces, -0.22, 0.18) * drawn
    return jnp.clip(drawn, min=-bound, max=bound).astype(kind)


def heavy_noise(key, extent, width, reach, cuts, heavy, kind=jnp.bfloat16):
    values = width * jax.random.normal(key, extent, jnp.float32)
    if cuts:
        values = values * level_of(key, extent, cuts, -0.22, 0.18)
    return jnp.clip(strengthened(values, jax.random.fold_in(key, 3), *heavy), -reach, reach).astype(kind)


def setup_inputs(seed: int = 0) -> dict:
    arg_keys = jax.random.split(jax.random.key(seed), 7)
    query_act = bell_draw(arg_keys[0], (SEQ, CHANNELS), 1.0, 6.0, ((0, 16), (1, 2)))
    key_act = bell_draw(arg_keys[1], (SEQ, CHANNELS), 1.0, 6.0, ((0, 16), (1, 2)))
    value_act = bell_draw(arg_keys[2], (SEQ, CHANNELS), 1.0, 6.0, ((0, 16), (1, 2)))
    filters = bell_draw(arg_keys[3], (SEQ, CHANNELS), SEQ ** -0.5, 0.125, ((0, 16), (1, 2)))
    skip_scale = bell_draw(arg_keys[4], (CHANNELS,), 1.0, 4.0, ((0, 2),), jnp.float32)
    w_out = heavy_noise(arg_keys[5], (CHANNELS, D), CHANNELS ** -0.5, 0.25, ((0, 2),), (0, 1, 2, 2.0))
    return {"query_act": query_act, "key_act": key_act, "value_act": value_act, "filters": filters, "skip_scale": skip_scale, "w_out": w_out}


def reference(query_act, key_act, value_act, filters, skip_scale, w_out):
    gated_in = (key_act.astype(jnp.float32) * value_act.astype(jnp.float32)).astype(jnp.bfloat16)
    signal = gated_in.astype(jnp.float32)
    fft_length = 2 * SEQ
    spectrum = jnp.fft.rfft(signal, n=fft_length, axis=0) * jnp.fft.rfft(filters.astype(jnp.float32), n=fft_length, axis=0)
    convolved = jnp.fft.irfft(spectrum, n=fft_length, axis=0)[:SEQ]
    gated = (query_act.astype(jnp.float32) * (convolved + skip_scale[None, :] * signal)).astype(jnp.bfloat16)
    grouped = jnp.moveaxis(gated.reshape(SEQ, N_CHAN, CH_DEV), 1, 0)
    weights = w_out.reshape(N_CHAN, CH_DEV, D)

    def add_group(running, operands):
        columns, w_rows = operands
        partial_value = jnp.dot(columns, w_rows, preferred_element_type=jnp.float32).astype(jnp.bfloat16)
        return running + partial_value.astype(jnp.float32), None

    running, unused = lax.scan(add_group, jnp.zeros((SEQ, D), jnp.float32), (grouped, weights))
    return running.astype(jnp.bfloat16)
```

```python
import functools
import math

import jax
import jax.numpy as jnp
import numpy as np
from jax import lax
from jax.experimental import pallas as pl
from jax.experimental.pallas import tpu as pltpu
from jax.sharding import PartitionSpec as P

MESH = pl.DeviceIdType.MESH
TILE = 8


def tables(block):
    pos = np.arange(block)
    angle = 2.0 * math.pi * np.outer(pos, pos + 0.25) / block
    forward = np.concatenate([np.cos(angle), -np.sin(angle)], axis=1)
    cos, sin = np.cos(angle).T / block, np.sin(angle).T / block
    inverse = np.block([[cos, -sin], [-sin, -cos]])
    return jnp.asarray(forward, jnp.bfloat16), jnp.asarray(inverse, jnp.bfloat16)


def kernel(
    n_ctx, n_chan, chunk,
    query_ref, key_ref, value_ref, filter_ref, skip_ref, fwd_ref, inv_ref, w_ref,
    out_ref,
    send, recv, spec, prod, back_send, back_recv, w_vmem, part_send, part_recv, own_part,
    send_sem, recv_sem, back_send_sem, back_recv_sem, part_send_sem, part_recv_sem, w_sem,
):
    me = lax.axis_index("ctx")
    my_chan = lax.axis_index("chan")
    block, width = key_ref.shape
    chans = width // n_ctx
    groups = chans // TILE
    feats = out_ref.shape[1]
    chunks = feats // chunk

    barrier = pltpu.get_barrier_semaphore()

    @pl.loop(1, n_ctx)
    def _(step):
        pl.semaphore_signal(barrier, inc=1, device_id={"ctx": lax.rem(me + step, n_ctx)}, device_id_type=MESH)

    @pl.loop(1, n_chan)
    def _(step):
        pl.semaphore_signal(barrier, inc=1, device_id={"chan": lax.rem(my_chan + step, n_chan)}, device_id_type=MESH)

    w_copy = pltpu.make_async_copy(w_ref, w_vmem, w_sem)
    w_copy.start()

    gated_in = (key_ref[...].astype(jnp.float32) * value_ref[...].astype(jnp.float32)).astype(jnp.bfloat16).astype(jnp.float32)
    signal_t = gated_in.T.reshape(n_ctx, chans, block)
    filter_t = filter_ref[...].astype(jnp.float32).T.reshape(n_ctx, chans, block)
    send[...] = jnp.concatenate([signal_t, filter_t], axis=1).astype(jnp.bfloat16)

    pl.semaphore_wait(barrier, n_ctx + n_chan - 2)

    def out_copy(peer):
        return pltpu.make_async_remote_copy(
            src_ref=send.at[peer], dst_ref=recv.at[me],
            send_sem=send_sem.at[peer], recv_sem=recv_sem.at[me],
            device_id={"ctx": peer}, device_id_type=MESH)

    def in_copy(peer):
        return pltpu.make_async_remote_copy(
            src_ref=send.at[me], dst_ref=recv.at[peer],
            send_sem=send_sem.at[me], recv_sem=recv_sem.at[peer],
            device_id={"ctx": peer}, device_id_type=MESH)

    @pl.loop(1, n_ctx)
    def _(step):
        out_copy(lax.rem(me + step, n_ctx)).start()

    recv[me] = send[me]

    @pl.loop(1, n_ctx)
    def _(step):
        in_copy(lax.rem(me + step, n_ctx)).wait_recv()

    spec[...] = jnp.dot(
        recv[...].reshape(n_ctx * 2 * chans, block), fwd_ref[...], preferred_element_type=jnp.float32
    ).reshape(n_ctx, 2 * groups, TILE, 2 * block)

    low, high = pl.ds(0, block), pl.ds(block, block)

    @pl.loop(0, groups)
    def _(group):
        @pl.loop(0, n_ctx // TILE)
        def _(tile):
            def accumulate(first, lag, acc, diagonal):
                acc = list(acc)
                lags = {}
                for i in range(0 if diagonal else 1 - TILE, TILE):
                    lags[i] = (spec[lag + i, groups + group, :, low], spec[lag + i, groups + group, :, high])
                for j in range(TILE):
                    real, imag = spec[first + j, group, :, low], spec[first + j, group, :, high]
                    for i in range(j if diagonal else 0, TILE):
                        f_real, f_imag = lags[i - j]
                        acc[2 * i] = acc[2 * i] + (real * f_real - imag * f_imag)
                        acc[2 * i + 1] = acc[2 * i + 1] + (real * f_imag + imag * f_real)
                return tuple(acc)

            zero = jnp.zeros((TILE, block), jnp.float32)
            acc = accumulate(tile * TILE, 0, (zero,) * (2 * TILE), True)
            acc = lax.fori_loop(
                0, tile, lambda u, acc: accumulate(u * TILE, (tile - u) * TILE, acc, False), acc)
            for i in range(TILE):
                prod[tile * TILE + i, group, :, low] = acc[2 * i]
                prod[tile * TILE + i, group, :, high] = acc[2 * i + 1]

    mixed = jnp.dot(
        prod[...].reshape(n_ctx * chans, 2 * block).astype(jnp.bfloat16), inv_ref[...],
        preferred_element_type=jnp.float32)
    first, carry = mixed[:, :block], mixed[:, block:]
    shifted = jnp.concatenate([jnp.zeros((chans, block), jnp.float32), carry[:-chans]], axis=0)
    back_send[...] = (first + shifted).reshape(n_ctx, chans, block).astype(jnp.bfloat16)

    def back_out(peer):
        return pltpu.make_async_remote_copy(
            src_ref=back_send.at[peer], dst_ref=back_recv.at[me],
            send_sem=back_send_sem.at[peer], recv_sem=back_recv_sem.at[me],
            device_id={"ctx": peer}, device_id_type=MESH)

    def back_in(peer):
        return pltpu.make_async_remote_copy(
            src_ref=back_send.at[me], dst_ref=back_recv.at[peer],
            send_sem=back_send_sem.at[me], recv_sem=back_recv_sem.at[peer],
            device_id={"ctx": peer}, device_id_type=MESH)

    @pl.loop(1, n_ctx)
    def _(step):
        back_out(lax.rem(me + step, n_ctx)).start()

    back_recv[me] = back_send[me]
    w_copy.wait()

    @pl.loop(1, n_ctx)
    def _(step):
        back_in(lax.rem(me + step, n_ctx)).wait_recv()

    convolved = back_recv[...].astype(jnp.float32).reshape(width, block).T
    signal = (key_ref[...].astype(jnp.float32) * value_ref[...].astype(jnp.float32)).astype(jnp.bfloat16).astype(jnp.float32)
    gated = (query_ref[...].astype(jnp.float32) * (convolved + skip_ref[...] * signal)).astype(jnp.bfloat16)

    def product(chan, piece):
        columns = pl.ds(pl.multiple_of(chan * feats + piece * chunk, chunk), chunk)
        return jnp.dot(gated, w_vmem[:, columns], preferred_element_type=jnp.float32)

    def part_out(chan, piece):
        return pltpu.make_async_remote_copy(
            src_ref=part_send.at[chan, piece], dst_ref=part_recv.at[my_chan, piece],
            send_sem=part_send_sem.at[chan, piece], recv_sem=part_recv_sem.at[my_chan, piece],
            device_id={"chan": chan}, device_id_type=MESH)

    def part_in(chan, piece):
        return pltpu.make_async_remote_copy(
            src_ref=part_send.at[my_chan, piece], dst_ref=part_recv.at[chan, piece],
            send_sem=part_send_sem.at[my_chan, piece], recv_sem=part_recv_sem.at[chan, piece],
            device_id={"chan": chan}, device_id_type=MESH)

    @pl.loop(1, n_chan)
    def _(step):
        chan = lax.rem(my_chan + step, n_chan)

        @pl.loop(0, chunks)
        def _(piece):
            part_send[chan, piece] = product(chan, piece).astype(jnp.bfloat16)
            part_out(chan, piece).start()

    @pl.loop(0, chunks)
    def _(piece):
        own_part[piece] = product(my_chan, piece).astype(jnp.bfloat16).astype(jnp.float32)

    for piece in range(chunks):
        def add(step, total):
            chan = lax.rem(my_chan + step, n_chan)
            part_in(chan, piece).wait_recv()
            return total + part_recv[chan, piece].astype(jnp.float32)
        out_ref[:, piece * chunk:(piece + 1) * chunk] = lax.fori_loop(
            1, n_chan, add, own_part[piece]).astype(jnp.bfloat16)

    @pl.loop(1, n_ctx)
    def _(step):
        peer = lax.rem(me + step, n_ctx)
        out_copy(peer).wait_send()
        back_out(peer).wait_send()

    @pl.loop(1, n_chan)
    def _(step):
        chan = lax.rem(my_chan + step, n_chan)

        @pl.loop(0, chunks)
        def _(piece):
            part_out(chan, piece).wait_send()


def shards(n_ctx, n_chan, query_act, key_act, value_act, filters, skip_scale, w_out):
    block, width = key_act.shape
    feats = w_out.shape[1] // n_chan
    chans = width // n_ctx
    chunk = min(512, feats)
    chunks = feats // chunk
    forward, inverse = tables(block)
    vmem = pl.BlockSpec(memory_space=pltpu.VMEM)
    dma = pltpu.SemaphoreType.DMA
    return pl.pallas_call(
        functools.partial(kernel, n_ctx, n_chan, chunk),
        out_shape=jax.ShapeDtypeStruct((block, feats), jnp.bfloat16),
        in_specs=[vmem] * 7 + [pl.BlockSpec(memory_space=pl.ANY)],
        out_specs=vmem,
        scratch_shapes=[
            pltpu.VMEM((n_ctx, 2 * chans, block), jnp.bfloat16),
            pltpu.VMEM((n_ctx, 2 * chans, block), jnp.bfloat16),
            pltpu.VMEM((n_ctx, 2 * chans // TILE, TILE, 2 * block), jnp.float32),
            pltpu.VMEM((n_ctx, chans // TILE, TILE, 2 * block), jnp.float32),
            pltpu.VMEM((n_ctx, chans, block), jnp.bfloat16),
            pltpu.VMEM((n_ctx, chans, block), jnp.bfloat16),
            pltpu.VMEM(w_out.shape, jnp.bfloat16),
            pltpu.VMEM((n_chan, chunks, block, chunk), jnp.bfloat16),
            pltpu.VMEM((n_chan, chunks, block, chunk), jnp.bfloat16),
            pltpu.VMEM((chunks, block, chunk), jnp.float32),
            dma((n_ctx,)), dma((n_ctx,)), dma((n_ctx,)), dma((n_ctx,)),
            dma((n_chan, chunks)), dma((n_chan, chunks)), dma,
        ],
        compiler_params=pltpu.CompilerParams(
            collective_id=0, has_side_effects=True, vmem_limit_bytes=40 * 1024 * 1024),
    )(query_act, key_act, value_act, filters, skip_scale.reshape(1, width), forward, inverse, w_out)


def solution(mesh):
    return jax.shard_map(
        functools.partial(shards, mesh.shape["ctx"], mesh.shape["chan"]),
        mesh=mesh,
        in_specs=(
            P("ctx", "chan"),
            P("ctx", "chan"),
            P("ctx", "chan"),
            P("ctx", "chan"),
            P("chan"),
            P("chan", None),
        ),
        out_specs=P("ctx", "chan"),
        check_vma=False,
    )
```

```python
import functools
import math

import jax
import jax.numpy as jnp
import numpy as np
from jax import lax
from jax.experimental import pallas as pl
from jax.experimental.pallas import tpu as pltpu
from jax.sharding import PartitionSpec as P

MESH = pl.DeviceIdType.MESH
TILE = 8
LANES = 128
PIECES = 4
AHEAD = 3


def tables(block):
    pos = np.arange(block)
    angle = 2.0 * math.pi * np.outer(pos, pos + 0.25) / block
    forward = np.concatenate([np.cos(angle), -np.sin(angle)], axis=1)
    cos, sin = np.cos(angle).T / block, np.sin(angle).T / block
    inverse = np.block([[cos, -sin], [-sin, -cos]])
    return jnp.asarray(forward, jnp.bfloat16), jnp.asarray(inverse, jnp.bfloat16)


def kernel(
    n_ctx, n_chan,
    query_hbm, key_hbm, value_hbm, filter_hbm, skip_hbm, fwd_hbm, inv_hbm, w_ref,
    out_ref,
    query_ref, key_ref, value_ref, filter_ref, skip_ref, fwd_ref, inv_ref,
    send, recv, spec, prod, back_send, back_recv, w_vmem, w_other, gated, gated_recv, part_send, part_recv, own_part,
    send_sem, recv_sem, back_send_sem, back_recv_sem, part_send_sem, part_recv_sem, load_sem,
    w_send_sem, w_recv_sem, pair_send_sem, pair_recv_sem, gated_send_sem, gated_recv_sem,
):
    me = lax.axis_index("ctx")
    my_chan = lax.axis_index("chan")
    block, width = key_ref.shape
    loads = [
        pltpu.make_async_copy(source, target, load_sem.at[i])
        for i, (source, target) in enumerate([
            (key_hbm, key_ref), (value_hbm, value_ref), (filter_hbm, filter_ref), (fwd_hbm, fwd_ref),
            (inv_hbm, inv_ref), (query_hbm, query_ref), (skip_hbm, skip_ref), (w_ref, w_vmem)])
    ]
    for load in loads:
        load.start()
    chans = width // n_ctx
    groups = chans // TILE
    feats = out_ref.shape[1]
    chunk = feats // PIECES
    ahead = AHEAD * chunk
    core = lax.rem(me, 2)
    sibling = me + 1 - 2 * core
    w_rows = width // 2 // PIECES

    def other(step):
        return lax.rem(my_chan + step, n_chan)

    def row_range(half, piece):
        return pl.ds(pl.multiple_of(half * (width // 2) + piece * w_rows, w_rows), w_rows)

    def w_move(chan, source, piece):
        rows = row_range(core, piece)
        return pltpu.make_async_remote_copy(
            src_ref=w_ref.at[rows, pl.ds(pl.multiple_of(chan * feats, chunk), ahead)],
            dst_ref=w_other.at[source, rows, :],
            send_sem=w_send_sem.at[chan, piece], recv_sem=w_recv_sem.at[source, piece],
            device_id={"chan": chan}, device_id_type=MESH)

    def pair_move(chan, half, piece):
        rows = row_range(half, piece)
        return pltpu.make_async_remote_copy(
            src_ref=w_other.at[chan, rows, :], dst_ref=w_other.at[chan, rows, :],
            send_sem=pair_send_sem.at[chan, piece], recv_sem=pair_recv_sem.at[chan, piece],
            device_id={"ctx": sibling}, device_id_type=MESH)

    def hand_over(piece):
        @pl.loop(1, n_chan)
        def _(step):
            chan = other(step)
            w_move(chan, chan, piece).wait_recv()
            pair_move(chan, core, piece).start()

    def gated_move(chan, source, piece):
        columns = pl.ds(piece * LANES, LANES)
        return pltpu.make_async_remote_copy(
            src_ref=gated.at[:, columns], dst_ref=gated_recv.at[source, :, columns],
            send_sem=gated_send_sem.at[chan, piece], recv_sem=gated_recv_sem.at[source, piece],
            device_id={"chan": chan}, device_id_type=MESH)

    barrier = pltpu.get_barrier_semaphore()

    @pl.loop(1, n_ctx)
    def _(step):
        pl.semaphore_signal(barrier, inc=1, device_id={"ctx": lax.rem(me + step, n_ctx)}, device_id_type=MESH)

    @pl.loop(1, n_chan)
    def _(step):
        pl.semaphore_signal(barrier, inc=1, device_id={"chan": lax.rem(my_chan + step, n_chan)}, device_id_type=MESH)

    for load in loads[:3]:
        load.wait()
    gated_in = (key_ref[...].astype(jnp.float32) * value_ref[...].astype(jnp.float32)).astype(jnp.bfloat16).astype(jnp.float32)
    signal_t = gated_in.T.reshape(n_ctx, chans, block)
    filter_t = filter_ref[...].astype(jnp.float32).T.reshape(n_ctx, chans, block)
    send[...] = jnp.concatenate([signal_t, filter_t], axis=1).astype(jnp.bfloat16)

    pl.semaphore_wait(barrier, n_ctx + n_chan - 2)

    def out_copy(peer):
        return pltpu.make_async_remote_copy(
            src_ref=send.at[peer], dst_ref=recv.at[me],
            send_sem=send_sem.at[peer], recv_sem=recv_sem.at[me],
            device_id={"ctx": peer}, device_id_type=MESH)

    def in_copy(peer):
        return pltpu.make_async_remote_copy(
            src_ref=send.at[me], dst_ref=recv.at[peer],
            send_sem=send_sem.at[me], recv_sem=recv_sem.at[peer],
            device_id={"ctx": peer}, device_id_type=MESH)

    @pl.loop(1, n_ctx)
    def _(step):
        out_copy(lax.rem(me + step, n_ctx)).start()

    @pl.loop(1, n_chan)
    def _(step):
        chan = other(step)

        @pl.loop(0, PIECES)
        def _(piece):
            w_move(chan, my_chan, piece).start()

    recv[me] = send[me]

    @pl.loop(1, n_ctx)
    def _(step):
        in_copy(lax.rem(me + step, n_ctx)).wait_recv()

    loads[3].wait()
    spec[...] = jnp.dot(
        recv[...].reshape(n_ctx * 2 * chans, block), fwd_ref[...], preferred_element_type=jnp.float32
    ).reshape(n_ctx, 2 * groups, TILE, 2 * block)

    low, high = pl.ds(0, block), pl.ds(block, block)

    @pl.loop(0, groups)
    def _(group):
        @pl.loop(0, n_ctx // TILE)
        def _(tile):
            def accumulate(first, lag, acc, diagonal):
                acc = list(acc)
                lags = {}
                for i in range(0 if diagonal else 1 - TILE, TILE):
                    lags[i] = (spec[lag + i, groups + group, :, low], spec[lag + i, groups + group, :, high])
                for j in range(TILE):
                    real, imag = spec[first + j, group, :, low], spec[first + j, group, :, high]
                    for i in range(j if diagonal else 0, TILE):
                        f_real, f_imag = lags[i - j]
                        acc[2 * i] = acc[2 * i] + (real * f_real - imag * f_imag)
                        acc[2 * i + 1] = acc[2 * i + 1] + (real * f_imag + imag * f_real)
                return tuple(acc)

            zero = jnp.zeros((TILE, block), jnp.float32)
            acc = accumulate(tile * TILE, 0, (zero,) * (2 * TILE), True)
            acc = lax.fori_loop(
                0, tile, lambda u, acc: accumulate(u * TILE, (tile - u) * TILE, acc, False), acc)
            for i in range(TILE):
                prod[tile * TILE + i, group, :, low] = acc[2 * i]
                prod[tile * TILE + i, group, :, high] = acc[2 * i + 1]

    hand_over(0)
    loads[4].wait()
    mixed = jnp.dot(
        prod[...].reshape(n_ctx * chans, 2 * block).astype(jnp.bfloat16), inv_ref[...],
        preferred_element_type=jnp.float32)
    first, carry = mixed[:, :block], mixed[:, block:]
    shifted = jnp.concatenate([jnp.zeros((chans, block), jnp.float32), carry[:-chans]], axis=0)
    back_send[...] = (first + shifted).reshape(n_ctx, chans, block).astype(jnp.bfloat16)

    def back_out(peer):
        return pltpu.make_async_remote_copy(
            src_ref=back_send.at[peer], dst_ref=back_recv.at[me],
            send_sem=back_send_sem.at[peer], recv_sem=back_recv_sem.at[me],
            device_id={"ctx": peer}, device_id_type=MESH)

    def back_in(peer):
        return pltpu.make_async_remote_copy(
            src_ref=back_send.at[me], dst_ref=back_recv.at[peer],
            send_sem=back_send_sem.at[me], recv_sem=back_recv_sem.at[peer],
            device_id={"ctx": peer}, device_id_type=MESH)

    @pl.loop(1, n_ctx)
    def _(step):
        back_out(lax.rem(me + step, n_ctx)).start()

    back_recv[me] = back_send[me]
    for load in loads[5:]:
        load.wait()
    hand_over(1)

    lots = width // LANES
    peers = n_ctx // lots
    for lot in range(lots):
        for peer in range(lot * peers, (lot + 1) * peers):
            @pl.when(peer != me)
            def _():
                back_in(peer).wait_recv()
        lanes = slice(lot * LANES, (lot + 1) * LANES)
        convolved = back_recv[lot * peers:(lot + 1) * peers].astype(jnp.float32).reshape(LANES, block).T
        signal = (key_ref[:, lanes].astype(jnp.float32) * value_ref[:, lanes].astype(jnp.float32)).astype(jnp.bfloat16).astype(jnp.float32)
        gated[:, lanes] = (
            query_ref[:, lanes].astype(jnp.float32) * (convolved + skip_ref[:, lanes] * signal)).astype(jnp.bfloat16)

        @pl.loop(1, n_chan)
        def _(step):
            gated_move(other(step), my_chan, lot).start()

    def product(chan, piece):
        columns = pl.ds(pl.multiple_of(chan * feats + piece * chunk, chunk), chunk)
        return jnp.dot(gated[...], w_vmem[:, columns], preferred_element_type=jnp.float32)

    def part_move(chan, source, piece):
        return pltpu.make_async_remote_copy(
            src_ref=part_send.at[chan, piece], dst_ref=part_recv.at[source, piece],
            send_sem=part_send_sem.at[chan, piece], recv_sem=part_recv_sem.at[source, piece],
            device_id={"chan": chan}, device_id_type=MESH)

    @pl.loop(1, n_chan)
    def _(step):
        chan = other(step)
        for piece in range(PIECES - AHEAD):
            part_send[chan, piece] = product(chan, AHEAD + piece).astype(jnp.bfloat16)
            part_move(chan, my_chan, piece).start()

    for piece in range(2, PIECES):
        hand_over(piece)

    for piece in range(PIECES):
        own_part[piece] = product(my_chan, piece)

    @pl.loop(1, n_chan)
    def _(step):
        chan = other(step)
        for piece in range(PIECES):
            pair_move(chan, 1 - core, piece).wait_recv()
        for lot in range(lots):
            gated_move(chan, chan, lot).wait_recv()

    for piece in range(AHEAD):
        columns = slice(piece * chunk, (piece + 1) * chunk)

        def gather(step, total):
            chan = other(step)
            return total + jnp.dot(
                gated_recv[chan], w_other[chan, :, columns], preferred_element_type=jnp.float32)
        out_ref[:, columns] = lax.fori_loop(1, n_chan, gather, own_part[piece]).astype(jnp.bfloat16)

    for piece in range(PIECES - AHEAD):
        columns = slice((AHEAD + piece) * chunk, (AHEAD + piece + 1) * chunk)

        def add(step, total):
            chan = other(step)
            part_move(chan, chan, piece).wait_recv()
            return total + part_recv[chan, piece].astype(jnp.float32)
        out_ref[:, columns] = lax.fori_loop(1, n_chan, add, own_part[AHEAD + piece]).astype(jnp.bfloat16)

    @pl.loop(1, n_ctx)
    def _(step):
        peer = lax.rem(me + step, n_ctx)
        out_copy(peer).wait_send()
        back_out(peer).wait_send()

    @pl.loop(1, n_chan)
    def _(step):
        chan = other(step)
        for piece in range(PIECES):
            w_move(chan, my_chan, piece).wait_send()
            pair_move(chan, core, piece).wait_send()
        for lot in range(lots):
            gated_move(chan, my_chan, lot).wait_send()
        for piece in range(PIECES - AHEAD):
            part_move(chan, my_chan, piece).wait_send()


def shards(n_ctx, n_chan, query_act, key_act, value_act, filters, skip_scale, w_out):
    block, width = key_act.shape
    feats = w_out.shape[1] // n_chan
    chans = width // n_ctx
    chunk = feats // PIECES
    rest = PIECES - AHEAD
    lots = width // LANES
    forward, inverse = tables(block)
    vmem = pl.BlockSpec(memory_space=pltpu.VMEM)
    dma = pltpu.SemaphoreType.DMA
    return pl.pallas_call(
        functools.partial(kernel, n_ctx, n_chan),
        out_shape=jax.ShapeDtypeStruct((block, feats), jnp.bfloat16),
        in_specs=[pl.BlockSpec(memory_space=pltpu.HBM)] * 8,
        out_specs=vmem,
        scratch_shapes=[pltpu.VMEM((block, width), jnp.bfloat16)] * 4 + [
            pltpu.VMEM((1, width), jnp.float32),
            pltpu.VMEM(forward.shape, jnp.bfloat16),
            pltpu.VMEM(inverse.shape, jnp.bfloat16),
            pltpu.VMEM((n_ctx, 2 * chans, block), jnp.bfloat16),
            pltpu.VMEM((n_ctx, 2 * chans, block), jnp.bfloat16),
            pltpu.VMEM((n_ctx, 2 * chans // TILE, TILE, 2 * block), jnp.float32),
            pltpu.VMEM((n_ctx, chans // TILE, TILE, 2 * block), jnp.float32),
            pltpu.VMEM((n_ctx, chans, block), jnp.bfloat16),
            pltpu.VMEM((n_ctx, chans, block), jnp.bfloat16),
            pltpu.VMEM(w_out.shape, jnp.bfloat16),
            pltpu.VMEM((n_chan, width, AHEAD * chunk), jnp.bfloat16),
            pltpu.VMEM((block, width), jnp.bfloat16),
            pltpu.VMEM((n_chan, block, width), jnp.bfloat16),
            pltpu.VMEM((n_chan, rest, block, chunk), jnp.bfloat16),
            pltpu.VMEM((n_chan, rest, block, chunk), jnp.bfloat16),
            pltpu.VMEM((PIECES, block, chunk), jnp.float32),
            dma((n_ctx,)), dma((n_ctx,)), dma((n_ctx,)), dma((n_ctx,)),
            dma((n_chan, rest)), dma((n_chan, rest)), dma((8,)),
            dma((n_chan, PIECES)), dma((n_chan, PIECES)), dma((n_chan, PIECES)), dma((n_chan, PIECES)),
            dma((n_chan, lots)), dma((n_chan, lots)),
        ],
        compiler_params=pltpu.CompilerParams(
            collective_id=0, has_side_effects=True, vmem_limit_bytes=62 * 1024 * 1024),
    )(query_act, key_act, value_act, filters, skip_scale.reshape(1, width), forward, inverse, w_out)


def solution(mesh):
    return jax.shard_map(
        functools.partial(shards, mesh.shape["ctx"], mesh.shape["chan"]),
        mesh=mesh,
        in_specs=(
            P("ctx", "chan"),
            P("ctx", "chan"),
            P("ctx", "chan"),
            P("ctx", "chan"),
            P("chan"),
            P("chan", None),
        ),
        out_specs=P("ctx", "chan"),
        check_vma=False,
    )
```

```python
import functools
import math

import jax
import jax.numpy as jnp
import numpy as np
from jax import lax
from jax.experimental import pallas as pl
from jax.experimental.pallas import tpu as pltpu
from jax.sharding import PartitionSpec as P

MESH = pl.DeviceIdType.MESH
TILE = 8
LANES = 128
PIECES = 4
AHEAD = 4
W_PIECES = 4


def tables(block):
    pos = np.arange(block)
    angle = 2.0 * math.pi * np.outer(pos, pos + 0.25) / block
    forward = np.concatenate([np.cos(angle), -np.sin(angle)], axis=1)
    cos, sin = np.cos(angle).T / block, np.sin(angle).T / block
    inverse = np.block([[cos, -sin], [-sin, -cos]])
    return jnp.asarray(forward, jnp.bfloat16), jnp.asarray(inverse, jnp.bfloat16)


def kernel(
    n_ctx, n_chan,
    query_hbm, key_hbm, value_hbm, filter_hbm, skip_hbm, fwd_hbm, inv_hbm, w_ref,
    out_ref,
    query_ref, key_ref, value_ref, filter_ref, skip_ref, fwd_ref, inv_ref,
    send, recv, spec, prod, back_send, back_recv, w_vmem, w_other, gated, gated_recv, part_send, part_recv, own_part,
    send_sem, recv_sem, back_send_sem, back_recv_sem, part_send_sem, part_recv_sem, load_sem,
    w_send_sem, w_recv_sem, side_send_sem, side_recv_sem, pair_send_sem, pair_recv_sem, gated_send_sem, gated_recv_sem,
):
    me = lax.axis_index("ctx")
    my_chan = lax.axis_index("chan")
    block, width = key_ref.shape
    loads = [
        pltpu.make_async_copy(source, target, load_sem.at[i])
        for i, (source, target) in enumerate([
            (key_hbm, key_ref), (value_hbm, value_ref), (filter_hbm, filter_ref), (fwd_hbm, fwd_ref),
            (inv_hbm, inv_ref), (query_hbm, query_ref), (skip_hbm, skip_ref), (w_ref, w_vmem)])
    ]
    for load in loads:
        load.start()
    chans = width // n_ctx
    groups = chans // TILE
    feats = out_ref.shape[1]
    chunk = feats // PIECES
    ahead = AHEAD * chunk
    core, side = lax.rem(me, 2), lax.rem(me // 2, 2)
    sibling, across = me + 1 - 2 * core, me + 2 - 4 * side
    quarter, far_quarter = 2 * side + core, 2 - 2 * side + core
    w_rows = width // 4 // W_PIECES

    def other(step):
        return lax.rem(my_chan + step, n_chan)

    def row_range(part, piece):
        return pl.ds(pl.multiple_of(part * (width // 4) + piece * w_rows, w_rows), w_rows)

    def w_move(chan, source, piece):
        rows = row_range(quarter, piece)
        return pltpu.make_async_remote_copy(
            src_ref=w_ref.at[rows, pl.ds(pl.multiple_of(chan * feats, chunk), ahead)],
            dst_ref=w_other.at[source, rows, :],
            send_sem=w_send_sem.at[chan, piece], recv_sem=w_recv_sem.at[source, piece],
            device_id={"chan": chan}, device_id_type=MESH)

    def side_move(chan, part, piece):
        rows = row_range(part, piece)
        return pltpu.make_async_remote_copy(
            src_ref=w_other.at[chan, rows, :], dst_ref=w_other.at[chan, rows, :],
            send_sem=side_send_sem.at[chan, piece], recv_sem=side_recv_sem.at[chan, piece],
            device_id={"ctx": across}, device_id_type=MESH)

    def pair_move(chan, part, piece, origin):
        rows = row_range(part, piece)
        return pltpu.make_async_remote_copy(
            src_ref=w_other.at[chan, rows, :], dst_ref=w_other.at[chan, rows, :],
            send_sem=pair_send_sem.at[chan, origin, piece], recv_sem=pair_recv_sem.at[chan, origin, piece],
            device_id={"ctx": sibling}, device_id_type=MESH)

    def hand_over(piece):
        @pl.loop(1, n_chan)
        def _(step):
            chan = other(step)
            w_move(chan, chan, piece).wait_recv()
            side_move(chan, quarter, piece).start()
            pair_move(chan, quarter, piece, 0).start()

    def hand_on(piece):
        @pl.loop(1, n_chan)
        def _(step):
            chan = other(step)
            side_move(chan, far_quarter, piece).wait_recv()
            pair_move(chan, far_quarter, piece, 1).start()

    def gated_move(chan, source, piece):
        columns = pl.ds(piece * LANES, LANES)
        return pltpu.make_async_remote_copy(
            src_ref=gated.at[:, columns], dst_ref=gated_recv.at[source, :, columns],
            send_sem=gated_send_sem.at[chan, piece], recv_sem=gated_recv_sem.at[source, piece],
            device_id={"chan": chan}, device_id_type=MESH)

    barrier = pltpu.get_barrier_semaphore()

    @pl.loop(1, n_ctx)
    def _(step):
        pl.semaphore_signal(barrier, inc=1, device_id={"ctx": lax.rem(me + step, n_ctx)}, device_id_type=MESH)

    @pl.loop(1, n_chan)
    def _(step):
        pl.semaphore_signal(barrier, inc=1, device_id={"chan": lax.rem(my_chan + step, n_chan)}, device_id_type=MESH)

    for load in loads[:3]:
        load.wait()
    gated_in = (key_ref[...].astype(jnp.float32) * value_ref[...].astype(jnp.float32)).astype(jnp.bfloat16).astype(jnp.float32)
    signal_t = gated_in.T.reshape(n_ctx, chans, block)
    filter_t = filter_ref[...].astype(jnp.float32).T.reshape(n_ctx, chans, block)
    send[...] = jnp.concatenate([signal_t, filter_t], axis=1).astype(jnp.bfloat16)

    pl.semaphore_wait(barrier, n_ctx + n_chan - 2)

    def out_copy(peer):
        return pltpu.make_async_remote_copy(
            src_ref=send.at[peer], dst_ref=recv.at[me],
            send_sem=send_sem.at[peer], recv_sem=recv_sem.at[me],
            device_id={"ctx": peer}, device_id_type=MESH)

    def in_copy(peer):
        return pltpu.make_async_remote_copy(
            src_ref=send.at[me], dst_ref=recv.at[peer],
            send_sem=send_sem.at[me], recv_sem=recv_sem.at[peer],
            device_id={"ctx": peer}, device_id_type=MESH)

    @pl.loop(1, n_ctx)
    def _(step):
        out_copy(lax.rem(me + step, n_ctx)).start()

    @pl.loop(1, n_chan)
    def _(step):
        chan = other(step)

        @pl.loop(0, W_PIECES)
        def _(piece):
            w_move(chan, my_chan, piece).start()

    recv[me] = send[me]
    hand_over(0)

    @pl.loop(1, n_ctx)
    def _(step):
        in_copy(lax.rem(me + step, n_ctx)).wait_recv()

    hand_over(1)
    loads[3].wait()
    spec[...] = jnp.dot(
        recv[...].reshape(n_ctx * 2 * chans, block), fwd_ref[...], preferred_element_type=jnp.float32
    ).reshape(n_ctx, 2 * groups, TILE, 2 * block)

    low, high = pl.ds(0, block), pl.ds(block, block)

    @pl.loop(0, groups)
    def _(group):
        @pl.loop(0, n_ctx // TILE)
        def _(tile):
            def accumulate(first, lag, acc, diagonal):
                acc = list(acc)
                lags = {}
                for i in range(0 if diagonal else 1 - TILE, TILE):
                    lags[i] = (spec[lag + i, groups + group, :, low], spec[lag + i, groups + group, :, high])
                for j in range(TILE):
                    real, imag = spec[first + j, group, :, low], spec[first + j, group, :, high]
                    for i in range(j if diagonal else 0, TILE):
                        f_real, f_imag = lags[i - j]
                        acc[2 * i] = acc[2 * i] + (real * f_real - imag * f_imag)
                        acc[2 * i + 1] = acc[2 * i + 1] + (real * f_imag + imag * f_real)
                return tuple(acc)

            zero = jnp.zeros((TILE, block), jnp.float32)
            acc = accumulate(tile * TILE, 0, (zero,) * (2 * TILE), True)
            acc = lax.fori_loop(
                0, tile, lambda u, acc: accumulate(u * TILE, (tile - u) * TILE, acc, False), acc)
            for i in range(TILE):
                prod[tile * TILE + i, group, :, low] = acc[2 * i]
                prod[tile * TILE + i, group, :, high] = acc[2 * i + 1]

    loads[4].wait()
    mixed = jnp.dot(
        prod[...].reshape(n_ctx * chans, 2 * block).astype(jnp.bfloat16), inv_ref[...],
        preferred_element_type=jnp.float32)
    first, carry = mixed[:, :block], mixed[:, block:]
    shifted = jnp.concatenate([jnp.zeros((chans, block), jnp.float32), carry[:-chans]], axis=0)
    back_send[...] = (first + shifted).reshape(n_ctx, chans, block).astype(jnp.bfloat16)

    def back_out(peer):
        return pltpu.make_async_remote_copy(
            src_ref=back_send.at[peer], dst_ref=back_recv.at[me],
            send_sem=back_send_sem.at[peer], recv_sem=back_recv_sem.at[me],
            device_id={"ctx": peer}, device_id_type=MESH)

    def back_in(peer):
        return pltpu.make_async_remote_copy(
            src_ref=back_send.at[me], dst_ref=back_recv.at[peer],
            send_sem=back_send_sem.at[me], recv_sem=back_recv_sem.at[peer],
            device_id={"ctx": peer}, device_id_type=MESH)

    @pl.loop(1, n_ctx)
    def _(step):
        back_out(lax.rem(me + step, n_ctx)).start()

    back_recv[me] = back_send[me]
    for load in loads[5:]:
        load.wait()
    for piece in range(2, W_PIECES):
        hand_over(piece)
    for piece in range(W_PIECES - 1):
        hand_on(piece)

    lots = width // LANES
    peers = n_ctx // lots
    for lot in range(lots):
        for peer in range(lot * peers, (lot + 1) * peers):
            @pl.when(peer != me)
            def _():
                back_in(peer).wait_recv()
        lanes = slice(lot * LANES, (lot + 1) * LANES)
        convolved = back_recv[lot * peers:(lot + 1) * peers].astype(jnp.float32).reshape(LANES, block).T
        signal = (key_ref[:, lanes].astype(jnp.float32) * value_ref[:, lanes].astype(jnp.float32)).astype(jnp.bfloat16).astype(jnp.float32)
        gated[:, lanes] = (
            query_ref[:, lanes].astype(jnp.float32) * (convolved + skip_ref[:, lanes] * signal)).astype(jnp.bfloat16)

        @pl.loop(1, n_chan)
        def _(step):
            gated_move(other(step), my_chan, lot).start()

    def product(chan, piece):
        columns = pl.ds(pl.multiple_of(chan * feats + piece * chunk, chunk), chunk)
        return jnp.dot(gated[...], w_vmem[:, columns], preferred_element_type=jnp.float32)

    def part_move(chan, source, piece):
        return pltpu.make_async_remote_copy(
            src_ref=part_send.at[chan, piece], dst_ref=part_recv.at[source, piece],
            send_sem=part_send_sem.at[chan, piece], recv_sem=part_recv_sem.at[source, piece],
            device_id={"chan": chan}, device_id_type=MESH)

    @pl.loop(1, n_chan)
    def _(step):
        chan = other(step)
        for piece in range(PIECES - AHEAD):
            part_send[chan, piece] = product(chan, AHEAD + piece).astype(jnp.bfloat16)
            part_move(chan, my_chan, piece).start()

    hand_on(W_PIECES - 1)

    for piece in range(PIECES):
        own_part[piece] = product(my_chan, piece)

    @pl.loop(1, n_chan)
    def _(step):
        chan = other(step)
        for piece in range(W_PIECES):
            pair_move(chan, 2 * side + 1 - core, piece, 0).wait_recv()
            pair_move(chan, 3 - 2 * side - core, piece, 1).wait_recv()
        for lot in range(lots):
            gated_move(chan, chan, lot).wait_recv()

    for piece in range(AHEAD):
        columns = slice(piece * chunk, (piece + 1) * chunk)

        def gather(step, total):
            chan = other(step)
            return total + jnp.dot(
                gated_recv[chan], w_other[chan, :, columns], preferred_element_type=jnp.float32)
        out_ref[:, columns] = lax.fori_loop(1, n_chan, gather, own_part[piece]).astype(jnp.bfloat16)

    for piece in range(PIECES - AHEAD):
        columns = slice((AHEAD + piece) * chunk, (AHEAD + piece + 1) * chunk)

        def add(step, total):
            chan = other(step)
            part_move(chan, chan, piece).wait_recv()
            return total + part_recv[chan, piece].astype(jnp.float32)
        out_ref[:, columns] = lax.fori_loop(1, n_chan, add, own_part[AHEAD + piece]).astype(jnp.bfloat16)

    @pl.loop(1, n_ctx)
    def _(step):
        peer = lax.rem(me + step, n_ctx)
        out_copy(peer).wait_send()
        back_out(peer).wait_send()

    @pl.loop(1, n_chan)
    def _(step):
        chan = other(step)
        for piece in range(W_PIECES):
            w_move(chan, my_chan, piece).wait_send()
            side_move(chan, quarter, piece).wait_send()
            pair_move(chan, quarter, piece, 0).wait_send()
            pair_move(chan, far_quarter, piece, 1).wait_send()
        for lot in range(lots):
            gated_move(chan, my_chan, lot).wait_send()
        for piece in range(PIECES - AHEAD):
            part_move(chan, my_chan, piece).wait_send()


def shards(n_ctx, n_chan, query_act, key_act, value_act, filters, skip_scale, w_out):
    block, width = key_act.shape
    feats = w_out.shape[1] // n_chan
    chans = width // n_ctx
    chunk = feats // PIECES
    rest = max(PIECES - AHEAD, 1)
    lots = width // LANES
    forward, inverse = tables(block)
    vmem = pl.BlockSpec(memory_space=pltpu.VMEM)
    dma = pltpu.SemaphoreType.DMA
    return pl.pallas_call(
        functools.partial(kernel, n_ctx, n_chan),
        out_shape=jax.ShapeDtypeStruct((block, feats), jnp.bfloat16),
        in_specs=[pl.BlockSpec(memory_space=pltpu.HBM)] * 8,
        out_specs=vmem,
        scratch_shapes=[pltpu.VMEM((block, width), jnp.bfloat16)] * 4 + [
            pltpu.VMEM((1, width), jnp.float32),
            pltpu.VMEM(forward.shape, jnp.bfloat16),
            pltpu.VMEM(inverse.shape, jnp.bfloat16),
            pltpu.VMEM((n_ctx, 2 * chans, block), jnp.bfloat16),
            pltpu.VMEM((n_ctx, 2 * chans, block), jnp.bfloat16),
            pltpu.VMEM((n_ctx, 2 * chans // TILE, TILE, 2 * block), jnp.float32),
            pltpu.VMEM((n_ctx, chans // TILE, TILE, 2 * block), jnp.float32),
            pltpu.VMEM((n_ctx, chans, block), jnp.bfloat16),
            pltpu.VMEM((n_ctx, chans, block), jnp.bfloat16),
            pltpu.VMEM(w_out.shape, jnp.bfloat16),
            pltpu.VMEM((n_chan, width, AHEAD * chunk), jnp.bfloat16),
            pltpu.VMEM((block, width), jnp.bfloat16),
            pltpu.VMEM((n_chan, block, width), jnp.bfloat16),
            pltpu.VMEM((n_chan, rest, block, chunk), jnp.bfloat16),
            pltpu.VMEM((n_chan, rest, block, chunk), jnp.bfloat16),
            pltpu.VMEM((PIECES, block, chunk), jnp.float32),
            dma((n_ctx,)), dma((n_ctx,)), dma((n_ctx,)), dma((n_ctx,)),
            dma((n_chan, rest)), dma((n_chan, rest)), dma((8,)),
            dma((n_chan, W_PIECES)), dma((n_chan, W_PIECES)), dma((n_chan, W_PIECES)), dma((n_chan, W_PIECES)),
            dma((n_chan, 2, W_PIECES)), dma((n_chan, 2, W_PIECES)),
            dma((n_chan, lots)), dma((n_chan, lots)),
        ],
        compiler_params=pltpu.CompilerParams(
            collective_id=0, has_side_effects=True, vmem_limit_bytes=62 * 1024 * 1024),
    )(query_act, key_act, value_act, filters, skip_scale.reshape(1, width), forward, inverse, w_out)


def solution(mesh):
    return jax.shard_map(
        functools.partial(shards, mesh.shape["ctx"], mesh.shape["chan"]),
        mesh=mesh,
        in_specs=(
            P("ctx", "chan"),
            P("ctx", "chan"),
            P("ctx", "chan"),
            P("ctx", "chan"),
            P("chan"),
            P("chan", None),
        ),
        out_specs=P("ctx", "chan"),
        check_vma=False,
    )
```

```python
import functools
import math

import jax
import jax.numpy as jnp
import numpy as np
from jax import lax
from jax.experimental import pallas as pl
from jax.experimental.pallas import tpu as pltpu
from jax.sharding import PartitionSpec as P

MESH = pl.DeviceIdType.MESH
TILE = 8
LANES = 128
PIECES = 4
AHEAD = 4
W_PIECES = 4


def tables(block):
    pos = np.arange(block)
    angle = 2.0 * math.pi * np.outer(pos, pos + 0.25) / block
    forward = np.concatenate([np.cos(angle), -np.sin(angle)], axis=1)
    cos, sin = np.cos(angle).T / block, np.sin(angle).T / block
    inverse = np.block([[cos, -sin], [-sin, -cos]])
    return jnp.asarray(forward, jnp.bfloat16), jnp.asarray(inverse, jnp.bfloat16)


def kernel(
    n_ctx, n_chan,
    query_hbm, key_hbm, value_hbm, filter_hbm, skip_hbm, fwd_hbm, inv_hbm, w_ref,
    out_ref,
    query_ref, key_ref, value_ref, filter_ref, skip_ref, fwd_ref, inv_ref,
    send, recv, spec, prod, back_send, back_recv, w_vmem, w_other, gated, gated_recv, part_send, part_recv, own_part,
    send_sem, recv_sem, back_send_sem, back_recv_sem, part_send_sem, part_recv_sem, load_sem,
    w_send_sem, w_recv_sem, side_send_sem, side_recv_sem, pair_send_sem, pair_recv_sem, gated_send_sem, gated_recv_sem, out_vmem, out_sem,
):
    me = lax.axis_index("ctx")
    my_chan = lax.axis_index("chan")
    block, width = key_ref.shape
    loads = [
        pltpu.make_async_copy(source, target, load_sem.at[i])
        for i, (source, target) in enumerate([
            (key_hbm, key_ref), (value_hbm, value_ref), (filter_hbm, filter_ref), (fwd_hbm, fwd_ref),
            (inv_hbm, inv_ref), (query_hbm, query_ref), (skip_hbm, skip_ref), (w_ref, w_vmem)])
    ]
    for load in loads:
        load.start()
    chans = width // n_ctx
    groups = chans // TILE
    feats = out_ref.shape[1]
    chunk = feats // PIECES
    ahead = AHEAD * chunk
    core, side = lax.rem(me, 2), lax.rem(me // 2, 2)
    sibling, across = me + 1 - 2 * core, me + 2 - 4 * side
    quarter, far_quarter = 2 * side + core, 2 - 2 * side + core
    w_rows = width // 4 // W_PIECES

    def other(step):
        return lax.rem(my_chan + step, n_chan)

    def row_range(part, piece):
        return pl.ds(pl.multiple_of(part * (width // 4) + piece * w_rows, w_rows), w_rows)

    def w_move(chan, source, piece):
        rows = row_range(quarter, piece)
        return pltpu.make_async_remote_copy(
            src_ref=w_ref.at[rows, pl.ds(pl.multiple_of(chan * feats, chunk), ahead)],
            dst_ref=w_other.at[source, rows, :],
            send_sem=w_send_sem.at[chan, piece], recv_sem=w_recv_sem.at[source, piece],
            device_id={"chan": chan}, device_id_type=MESH)

    def side_move(chan, part, piece):
        rows = row_range(part, piece)
        return pltpu.make_async_remote_copy(
            src_ref=w_other.at[chan, rows, :], dst_ref=w_other.at[chan, rows, :],
            send_sem=side_send_sem.at[chan, piece], recv_sem=side_recv_sem.at[chan, piece],
            device_id={"ctx": across}, device_id_type=MESH)

    def pair_move(chan, part, piece, origin):
        rows = row_range(part, piece)
        return pltpu.make_async_remote_copy(
            src_ref=w_other.at[chan, rows, :], dst_ref=w_other.at[chan, rows, :],
            send_sem=pair_send_sem.at[chan, origin, piece], recv_sem=pair_recv_sem.at[chan, origin, piece],
            device_id={"ctx": sibling}, device_id_type=MESH)

    def hand_over(piece):
        @pl.loop(1, n_chan)
        def _(step):
            chan = other(step)
            w_move(chan, chan, piece).wait_recv()
            side_move(chan, quarter, piece).start()
            pair_move(chan, quarter, piece, 0).start()

    def hand_on(piece):
        @pl.loop(1, n_chan)
        def _(step):
            chan = other(step)
            side_move(chan, far_quarter, piece).wait_recv()
            pair_move(chan, far_quarter, piece, 1).start()

    def gated_move(chan, source, piece):
        columns = pl.ds(piece * LANES, LANES)
        return pltpu.make_async_remote_copy(
            src_ref=gated.at[:, columns], dst_ref=gated_recv.at[source, :, columns],
            send_sem=gated_send_sem.at[chan, piece], recv_sem=gated_recv_sem.at[source, piece],
            device_id={"chan": chan}, device_id_type=MESH)

    barrier = pltpu.get_barrier_semaphore()

    @pl.loop(1, n_ctx)
    def _(step):
        pl.semaphore_signal(barrier, inc=1, device_id={"ctx": lax.rem(me + step, n_ctx)}, device_id_type=MESH)

    @pl.loop(1, n_chan)
    def _(step):
        pl.semaphore_signal(barrier, inc=1, device_id={"chan": lax.rem(my_chan + step, n_chan)}, device_id_type=MESH)

    for load in loads[:3]:
        load.wait()
    gated_in = (key_ref[...].astype(jnp.float32) * value_ref[...].astype(jnp.float32)).astype(jnp.bfloat16).astype(jnp.float32)
    signal_t = gated_in.T.reshape(n_ctx, chans, block)
    filter_t = filter_ref[...].astype(jnp.float32).T.reshape(n_ctx, chans, block)
    send[...] = jnp.concatenate([signal_t, filter_t], axis=1).astype(jnp.bfloat16)

    pl.semaphore_wait(barrier, n_ctx + n_chan - 2)

    def out_copy(peer):
        return pltpu.make_async_remote_copy(
            src_ref=send.at[peer], dst_ref=recv.at[me],
            send_sem=send_sem.at[peer], recv_sem=recv_sem.at[me],
            device_id={"ctx": peer}, device_id_type=MESH)

    def in_copy(peer):
        return pltpu.make_async_remote_copy(
            src_ref=send.at[me], dst_ref=recv.at[peer],
            send_sem=send_sem.at[me], recv_sem=recv_sem.at[peer],
            device_id={"ctx": peer}, device_id_type=MESH)

    @pl.loop(1, n_chan)
    def _(step):
        chan = other(step)

        @pl.loop(0, W_PIECES)
        def _(piece):
            w_move(chan, my_chan, piece).start()

    @pl.loop(1, n_ctx)
    def _(step):
        out_copy(lax.rem(me + step, n_ctx)).start()

    recv[me] = send[me]
    hand_over(0)

    @pl.loop(1, n_ctx)
    def _(step):
        in_copy(lax.rem(me + step, n_ctx)).wait_recv()

    hand_over(1)
    loads[3].wait()
    spec[...] = jnp.dot(
        recv[...].reshape(n_ctx * 2 * chans, block), fwd_ref[...], preferred_element_type=jnp.float32
    ).reshape(n_ctx, 2 * groups, TILE, 2 * block)

    low, high = pl.ds(0, block), pl.ds(block, block)

    @pl.loop(0, groups)
    def _(group):
        @pl.loop(0, n_ctx // TILE)
        def _(tile):
            def accumulate(first, lag, acc, diagonal):
                acc = list(acc)
                lags = {}
                for i in range(0 if diagonal else 1 - TILE, TILE):
                    lags[i] = (spec[lag + i, groups + group, :, low], spec[lag + i, groups + group, :, high])
                for j in range(TILE):
                    real, imag = spec[first + j, group, :, low], spec[first + j, group, :, high]
                    for i in range(j if diagonal else 0, TILE):
                        f_real, f_imag = lags[i - j]
                        acc[2 * i] = acc[2 * i] + (real * f_real - imag * f_imag)
                        acc[2 * i + 1] = acc[2 * i + 1] + (real * f_imag + imag * f_real)
                return tuple(acc)

            zero = jnp.zeros((TILE, block), jnp.float32)
            acc = accumulate(tile * TILE, 0, (zero,) * (2 * TILE), True)
            acc = lax.fori_loop(
                0, tile, lambda u, acc: accumulate(u * TILE, (tile - u) * TILE, acc, False), acc)
            for i in range(TILE):
                prod[tile * TILE + i, group, :, low] = acc[2 * i]
                prod[tile * TILE + i, group, :, high] = acc[2 * i + 1]

    loads[4].wait()
    mixed = jnp.dot(
        prod[...].reshape(n_ctx * chans, 2 * block).astype(jnp.bfloat16), inv_ref[...],
        preferred_element_type=jnp.float32)
    first, carry = mixed[:, :block], mixed[:, block:]
    shifted = jnp.concatenate([jnp.zeros((chans, block), jnp.float32), carry[:-chans]], axis=0)
    back_send[...] = (first + shifted).reshape(n_ctx, chans, block).astype(jnp.bfloat16)

    def back_out(peer):
        return pltpu.make_async_remote_copy(
            src_ref=back_send.at[peer], dst_ref=back_recv.at[me],
            send_sem=back_send_sem.at[peer], recv_sem=back_recv_sem.at[me],
            device_id={"ctx": peer}, device_id_type=MESH)

    def back_in(peer):
        return pltpu.make_async_remote_copy(
            src_ref=back_send.at[me], dst_ref=back_recv.at[peer],
            send_sem=back_send_sem.at[me], recv_sem=back_recv_sem.at[peer],
            device_id={"ctx": peer}, device_id_type=MESH)

    @pl.loop(1, n_ctx)
    def _(step):
        back_out(lax.rem(me + step, n_ctx)).start()

    back_recv[me] = back_send[me]
    for load in loads[5:]:
        load.wait()
    for piece in range(2, W_PIECES):
        hand_over(piece)

    lots = width // LANES
    peers = n_ctx // lots
    for lot in range(lots):
        for peer in range(lot * peers, (lot + 1) * peers):
            @pl.when(peer != me)
            def _():
                back_in(peer).wait_recv()
        lanes = slice(lot * LANES, (lot + 1) * LANES)
        convolved = back_recv[lot * peers:(lot + 1) * peers].astype(jnp.float32).reshape(LANES, block).T
        signal = (key_ref[:, lanes].astype(jnp.float32) * value_ref[:, lanes].astype(jnp.float32)).astype(jnp.bfloat16).astype(jnp.float32)
        gated[:, lanes] = (
            query_ref[:, lanes].astype(jnp.float32) * (convolved + skip_ref[:, lanes] * signal)).astype(jnp.bfloat16)

        @pl.loop(1, n_chan)
        def _(step):
            gated_move(other(step), my_chan, lot).start()

    def product(chan, piece):
        columns = pl.ds(pl.multiple_of(chan * feats + piece * chunk, chunk), chunk)
        return jnp.dot(gated[...], w_vmem[:, columns], preferred_element_type=jnp.float32)

    def part_move(chan, source, piece):
        return pltpu.make_async_remote_copy(
            src_ref=part_send.at[chan, piece], dst_ref=part_recv.at[source, piece],
            send_sem=part_send_sem.at[chan, piece], recv_sem=part_recv_sem.at[source, piece],
            device_id={"chan": chan}, device_id_type=MESH)

    @pl.loop(1, n_chan)
    def _(step):
        chan = other(step)
        for piece in range(PIECES - AHEAD):
            part_send[chan, piece] = product(chan, AHEAD + piece).astype(jnp.bfloat16)
            part_move(chan, my_chan, piece).start()

    for piece in range(W_PIECES):
        hand_on(piece)

    for piece in range(PIECES):
        own_part[piece] = product(my_chan, piece)

    @pl.loop(1, n_chan)
    def _(step):
        chan = other(step)
        for piece in range(W_PIECES):
            pair_move(chan, 2 * side + 1 - core, piece, 0).wait_recv()
            pair_move(chan, 3 - 2 * side - core, piece, 1).wait_recv()
        for lot in range(lots):
            gated_move(chan, chan, lot).wait_recv()

    def out_move(piece):
        columns = pl.ds(piece * chunk, chunk)
        return pltpu.make_async_copy(out_vmem.at[:, columns], out_ref.at[:, columns], out_sem.at[piece])

    for piece in range(AHEAD):
        columns = slice(piece * chunk, (piece + 1) * chunk)

        def gather(step, total):
            chan = other(step)
            return total + jnp.dot(
                gated_recv[chan], w_other[chan, :, columns], preferred_element_type=jnp.float32)
        out_vmem[:, columns] = lax.fori_loop(1, n_chan, gather, own_part[piece]).astype(jnp.bfloat16)
        out_move(piece).start()

    for piece in range(PIECES - AHEAD):
        columns = slice((AHEAD + piece) * chunk, (AHEAD + piece + 1) * chunk)

        def add(step, total):
            chan = other(step)
            part_move(chan, chan, piece).wait_recv()
            return total + part_recv[chan, piece].astype(jnp.float32)
        out_vmem[:, columns] = lax.fori_loop(1, n_chan, add, own_part[AHEAD + piece]).astype(jnp.bfloat16)
        out_move(AHEAD + piece).start()

    @pl.loop(1, n_ctx)
    def _(step):
        peer = lax.rem(me + step, n_ctx)
        out_copy(peer).wait_send()
        back_out(peer).wait_send()

    @pl.loop(1, n_chan)
    def _(step):
        chan = other(step)
        for piece in range(W_PIECES):
            w_move(chan, my_chan, piece).wait_send()
            side_move(chan, quarter, piece).wait_send()
            pair_move(chan, quarter, piece, 0).wait_send()
            pair_move(chan, far_quarter, piece, 1).wait_send()
        for lot in range(lots):
            gated_move(chan, my_chan, lot).wait_send()
        for piece in range(PIECES - AHEAD):
            part_move(chan, my_chan, piece).wait_send()

    for piece in range(PIECES):
        out_move(piece).wait()


def shards(n_ctx, n_chan, query_act, key_act, value_act, filters, skip_scale, w_out):
    block, width = key_act.shape
    feats = w_out.shape[1] // n_chan
    chans = width // n_ctx
    chunk = feats // PIECES
    rest = max(PIECES - AHEAD, 1)
    lots = width // LANES
    forward, inverse = tables(block)
    vmem = pl.BlockSpec(memory_space=pltpu.VMEM)
    dma = pltpu.SemaphoreType.DMA
    return pl.pallas_call(
        functools.partial(kernel, n_ctx, n_chan),
        out_shape=jax.ShapeDtypeStruct((block, feats), jnp.bfloat16),
        in_specs=[pl.BlockSpec(memory_space=pltpu.HBM)] * 8,
        out_specs=pl.BlockSpec(memory_space=pltpu.HBM),
        scratch_shapes=[pltpu.VMEM((block, width), jnp.bfloat16)] * 4 + [
            pltpu.VMEM((1, width), jnp.float32),
            pltpu.VMEM(forward.shape, jnp.bfloat16),
            pltpu.VMEM(inverse.shape, jnp.bfloat16),
            pltpu.VMEM((n_ctx, 2 * chans, block), jnp.bfloat16),
            pltpu.VMEM((n_ctx, 2 * chans, block), jnp.bfloat16),
            pltpu.VMEM((n_ctx, 2 * chans // TILE, TILE, 2 * block), jnp.float32),
            pltpu.VMEM((n_ctx, chans // TILE, TILE, 2 * block), jnp.float32),
            pltpu.VMEM((n_ctx, chans, block), jnp.bfloat16),
            pltpu.VMEM((n_ctx, chans, block), jnp.bfloat16),
            pltpu.VMEM(w_out.shape, jnp.bfloat16),
            pltpu.VMEM((n_chan, width, AHEAD * chunk), jnp.bfloat16),
            pltpu.VMEM((block, width), jnp.bfloat16),
            pltpu.VMEM((n_chan, block, width), jnp.bfloat16),
            pltpu.VMEM((n_chan, rest, block, chunk), jnp.bfloat16),
            pltpu.VMEM((n_chan, rest, block, chunk), jnp.bfloat16),
            pltpu.VMEM((PIECES, block, chunk), jnp.float32),
            dma((n_ctx,)), dma((n_ctx,)), dma((n_ctx,)), dma((n_ctx,)),
            dma((n_chan, rest)), dma((n_chan, rest)), dma((8,)),
            dma((n_chan, W_PIECES)), dma((n_chan, W_PIECES)), dma((n_chan, W_PIECES)), dma((n_chan, W_PIECES)),
            dma((n_chan, 2, W_PIECES)), dma((n_chan, 2, W_PIECES)),
            dma((n_chan, lots)), dma((n_chan, lots)),
            pltpu.VMEM((block, feats), jnp.bfloat16), dma((PIECES,)),
        ],
        compiler_params=pltpu.CompilerParams(
            collective_id=0, has_side_effects=True, vmem_limit_bytes=62 * 1024 * 1024),
    )(query_act, key_act, value_act, filters, skip_scale.reshape(1, width), forward, inverse, w_out)


def solution(mesh):
    return jax.shard_map(
        functools.partial(shards, mesh.shape["ctx"], mesh.shape["chan"]),
        mesh=mesh,
        in_specs=(
            P("ctx", "chan"),
            P("ctx", "chan"),
            P("ctx", "chan"),
            P("ctx", "chan"),
            P("chan"),
            P("chan", None),
        ),
        out_specs=P("ctx", "chan"),
        check_vma=False,
    )
```

```python
import functools
import math

import jax
import jax.numpy as jnp
import numpy as np
from jax import lax
from jax.experimental import pallas as pl
from jax.experimental.pallas import tpu as pltpu
from jax.sharding import PartitionSpec as P

MESH = pl.DeviceIdType.MESH
TILE = 8
LANES = 128
PIECES = 4
AHEAD = 3
W_PIECES = 4


def tables(block):
    pos = np.arange(block)
    angle = 2.0 * math.pi * np.outer(pos, pos + 0.25) / block
    forward = np.concatenate([np.cos(angle), -np.sin(angle)], axis=1)
    cos, sin = np.cos(angle).T / block, np.sin(angle).T / block
    inverse = np.block([[cos, -sin], [-sin, -cos]])
    return jnp.asarray(forward, jnp.bfloat16), jnp.asarray(inverse, jnp.bfloat16)


def kernel(
    n_ctx, n_chan,
    query_hbm, key_hbm, value_hbm, filter_hbm, skip_hbm, fwd_hbm, inv_hbm, w_ref,
    out_ref,
    query_ref, key_ref, value_ref, filter_ref, skip_ref, fwd_ref, inv_ref,
    send, recv, spec, prod, back_send, back_recv, w_vmem, w_other, gated, gated_recv, part_send, part_recv, own_part,
    send_sem, recv_sem, back_send_sem, back_recv_sem, part_send_sem, part_recv_sem, load_sem,
    w_send_sem, w_recv_sem, side_send_sem, side_recv_sem, pair_send_sem, pair_recv_sem, gated_send_sem, gated_recv_sem, out_vmem, out_sem,
):
    me = lax.axis_index("ctx")
    my_chan = lax.axis_index("chan")
    block, width = key_ref.shape
    loads = [
        pltpu.make_async_copy(source, target, load_sem.at[i])
        for i, (source, target) in enumerate([
            (key_hbm, key_ref), (value_hbm, value_ref), (filter_hbm, filter_ref), (fwd_hbm, fwd_ref),
            (inv_hbm, inv_ref), (query_hbm, query_ref), (skip_hbm, skip_ref), (w_ref, w_vmem)])
    ]
    for load in loads:
        load.start()
    chans = width // n_ctx
    groups = chans // TILE
    feats = out_ref.shape[1]
    chunk = feats // PIECES
    ahead = AHEAD * chunk
    core, side = lax.rem(me, 2), lax.rem(me // 2, 2)
    sibling, across = me + 1 - 2 * core, me + 2 - 4 * side
    quarter, far_quarter = 2 * side + core, 2 - 2 * side + core
    w_rows = width // 4 // W_PIECES

    def other(step):
        return lax.rem(my_chan + step, n_chan)

    def row_range(part, piece):
        return pl.ds(pl.multiple_of(part * (width // 4) + piece * w_rows, w_rows), w_rows)

    def w_move(chan, source, piece):
        rows = row_range(quarter, piece)
        return pltpu.make_async_remote_copy(
            src_ref=w_ref.at[rows, pl.ds(pl.multiple_of(chan * feats, chunk), ahead)],
            dst_ref=w_other.at[source, rows, :],
            send_sem=w_send_sem.at[chan, piece], recv_sem=w_recv_sem.at[source, piece],
            device_id={"chan": chan}, device_id_type=MESH)

    def side_move(chan, part, piece):
        rows = row_range(part, piece)
        return pltpu.make_async_remote_copy(
            src_ref=w_other.at[chan, rows, :], dst_ref=w_other.at[chan, rows, :],
            send_sem=side_send_sem.at[chan, piece], recv_sem=side_recv_sem.at[chan, piece],
            device_id={"ctx": across}, device_id_type=MESH)

    def pair_move(chan, part, piece, origin):
        rows = row_range(part, piece)
        return pltpu.make_async_remote_copy(
            src_ref=w_other.at[chan, rows, :], dst_ref=w_other.at[chan, rows, :],
            send_sem=pair_send_sem.at[chan, origin, piece], recv_sem=pair_recv_sem.at[chan, origin, piece],
            device_id={"ctx": sibling}, device_id_type=MESH)

    def hand_over(piece):
        @pl.loop(1, n_chan)
        def _(step):
            chan = other(step)
            w_move(chan, chan, piece).wait_recv()
            side_move(chan, quarter, piece).start()
            pair_move(chan, quarter, piece, 0).start()

    def hand_on(piece):
        @pl.loop(1, n_chan)
        def _(step):
            chan = other(step)
            side_move(chan, far_quarter, piece).wait_recv()
            pair_move(chan, far_quarter, piece, 1).start()

    def gated_move(chan, source, piece):
        columns = pl.ds(piece * LANES, LANES)
        return pltpu.make_async_remote_copy(
            src_ref=gated.at[:, columns], dst_ref=gated_recv.at[source, :, columns],
            send_sem=gated_send_sem.at[chan, piece], recv_sem=gated_recv_sem.at[source, piece],
            device_id={"chan": chan}, device_id_type=MESH)

    barrier = pltpu.get_barrier_semaphore()

    @pl.loop(1, n_ctx)
    def _(step):
        pl.semaphore_signal(barrier, inc=1, device_id={"ctx": lax.rem(me + step, n_ctx)}, device_id_type=MESH)

    @pl.loop(1, n_chan)
    def _(step):
        pl.semaphore_signal(barrier, inc=1, device_id={"chan": lax.rem(my_chan + step, n_chan)}, device_id_type=MESH)

    for load in loads[:3]:
        load.wait()
    gated_in = (key_ref[...].astype(jnp.float32) * value_ref[...].astype(jnp.float32)).astype(jnp.bfloat16).astype(jnp.float32)
    signal_t = gated_in.T.reshape(n_ctx, chans, block)
    filter_t = filter_ref[...].astype(jnp.float32).T.reshape(n_ctx, chans, block)
    send[...] = jnp.concatenate([signal_t, filter_t], axis=1).astype(jnp.bfloat16)

    pl.semaphore_wait(barrier, n_ctx + n_chan - 2)

    def out_copy(peer):
        return pltpu.make_async_remote_copy(
            src_ref=send.at[peer], dst_ref=recv.at[me],
            send_sem=send_sem.at[peer], recv_sem=recv_sem.at[me],
            device_id={"ctx": peer}, device_id_type=MESH)

    def in_copy(peer):
        return pltpu.make_async_remote_copy(
            src_ref=send.at[me], dst_ref=recv.at[peer],
            send_sem=send_sem.at[me], recv_sem=recv_sem.at[peer],
            device_id={"ctx": peer}, device_id_type=MESH)

    @pl.loop(1, n_chan)
    def _(step):
        chan = other(step)

        @pl.loop(0, W_PIECES)
        def _(piece):
            w_move(chan, my_chan, piece).start()

    @pl.loop(1, n_ctx)
    def _(step):
        out_copy(lax.rem(me + step, n_ctx)).start()

    recv[me] = send[me]
    hand_over(0)

    @pl.loop(1, n_ctx)
    def _(step):
        in_copy(lax.rem(me + step, n_ctx)).wait_recv()

    hand_over(1)
    loads[3].wait()
    spec[...] = jnp.dot(
        recv[...].reshape(n_ctx * 2 * chans, block), fwd_ref[...], preferred_element_type=jnp.float32
    ).reshape(n_ctx, 2 * groups, TILE, 2 * block)

    low, high = pl.ds(0, block), pl.ds(block, block)

    @pl.loop(0, groups)
    def _(group):
        @pl.loop(0, n_ctx // TILE)
        def _(tile):
            def accumulate(first, lag, acc, diagonal):
                acc = list(acc)
                lags = {}
                for i in range(0 if diagonal else 1 - TILE, TILE):
                    lags[i] = (spec[lag + i, groups + group, :, low], spec[lag + i, groups + group, :, high])
                for j in range(TILE):
                    real, imag = spec[first + j, group, :, low], spec[first + j, group, :, high]
                    for i in range(j if diagonal else 0, TILE):
                        f_real, f_imag = lags[i - j]
                        acc[2 * i] = acc[2 * i] + (real * f_real - imag * f_imag)
                        acc[2 * i + 1] = acc[2 * i + 1] + (real * f_imag + imag * f_real)
                return tuple(acc)

            zero = jnp.zeros((TILE, block), jnp.float32)
            acc = accumulate(tile * TILE, 0, (zero,) * (2 * TILE), True)
            acc = lax.fori_loop(
                0, tile, lambda u, acc: accumulate(u * TILE, (tile - u) * TILE, acc, False), acc)
            for i in range(TILE):
                prod[tile * TILE + i, group, :, low] = acc[2 * i]
                prod[tile * TILE + i, group, :, high] = acc[2 * i + 1]

    loads[4].wait()
    mixed = jnp.dot(
        prod[...].reshape(n_ctx * chans, 2 * block).astype(jnp.bfloat16), inv_ref[...],
        preferred_element_type=jnp.float32)
    first, carry = mixed[:, :block], mixed[:, block:]
    shifted = jnp.concatenate([jnp.zeros((chans, block), jnp.float32), carry[:-chans]], axis=0)
    back_send[...] = (first + shifted).reshape(n_ctx, chans, block).astype(jnp.bfloat16)

    def back_out(peer):
        return pltpu.make_async_remote_copy(
            src_ref=back_send.at[peer], dst_ref=back_recv.at[me],
            send_sem=back_send_sem.at[peer], recv_sem=back_recv_sem.at[me],
            device_id={"ctx": peer}, device_id_type=MESH)

    def back_in(peer):
        return pltpu.make_async_remote_copy(
            src_ref=back_send.at[me], dst_ref=back_recv.at[peer],
            send_sem=back_send_sem.at[me], recv_sem=back_recv_sem.at[peer],
            device_id={"ctx": peer}, device_id_type=MESH)

    @pl.loop(1, n_ctx)
    def _(step):
        back_out(lax.rem(me + step, n_ctx)).start()

    back_recv[me] = back_send[me]
    for load in loads[5:]:
        load.wait()
    for piece in range(2, W_PIECES):
        hand_over(piece)

    lots = width // LANES
    peers = n_ctx // lots
    for lot in range(lots):
        for peer in range(lot * peers, (lot + 1) * peers):
            @pl.when(peer != me)
            def _():
                back_in(peer).wait_recv()
        lanes = slice(lot * LANES, (lot + 1) * LANES)
        convolved = back_recv[lot * peers:(lot + 1) * peers].astype(jnp.float32).reshape(LANES, block).T
        signal = (key_ref[:, lanes].astype(jnp.float32) * value_ref[:, lanes].astype(jnp.float32)).astype(jnp.bfloat16).astype(jnp.float32)
        gated[:, lanes] = (
            query_ref[:, lanes].astype(jnp.float32) * (convolved + skip_ref[:, lanes] * signal)).astype(jnp.bfloat16)

        @pl.loop(1, n_chan)
        def _(step):
            gated_move(other(step), my_chan, lot).start()

    def product(chan, piece):
        columns = pl.ds(pl.multiple_of(chan * feats + piece * chunk, chunk), chunk)
        return jnp.dot(gated[...], w_vmem[:, columns], preferred_element_type=jnp.float32)

    def part_move(chan, source, piece):
        return pltpu.make_async_remote_copy(
            src_ref=part_send.at[chan, piece], dst_ref=part_recv.at[source, piece],
            send_sem=part_send_sem.at[chan, piece], recv_sem=part_recv_sem.at[source, piece],
            device_id={"chan": chan}, device_id_type=MESH)

    @pl.loop(1, n_chan)
    def _(step):
        chan = other(step)
        for piece in range(PIECES - AHEAD):
            part_send[chan, piece] = product(chan, AHEAD + piece).astype(jnp.bfloat16)
            part_move(chan, my_chan, piece).start()

    for piece in range(W_PIECES):
        hand_on(piece)

    for piece in range(PIECES):
        own_part[piece] = product(my_chan, piece)

    @pl.loop(1, n_chan)
    def _(step):
        chan = other(step)
        for piece in range(W_PIECES):
            pair_move(chan, 2 * side + 1 - core, piece, 0).wait_recv()
            pair_move(chan, 3 - 2 * side - core, piece, 1).wait_recv()
        for lot in range(lots):
            gated_move(chan, chan, lot).wait_recv()

    def out_move(piece):
        columns = pl.ds(piece * chunk, chunk)
        return pltpu.make_async_copy(out_vmem.at[:, columns], out_ref.at[:, columns], out_sem.at[piece])

    for piece in range(AHEAD):
        columns = slice(piece * chunk, (piece + 1) * chunk)

        def gather(step, total):
            chan = other(step)
            return total + jnp.dot(
                gated_recv[chan], w_other[chan, :, columns], preferred_element_type=jnp.float32)
        out_vmem[:, columns] = lax.fori_loop(1, n_chan, gather, own_part[piece]).astype(jnp.bfloat16)
        out_move(piece).start()

    for piece in range(PIECES - AHEAD):
        columns = slice((AHEAD + piece) * chunk, (AHEAD + piece + 1) * chunk)

        def add(step, total):
            chan = other(step)
            part_move(chan, chan, piece).wait_recv()
            return total + part_recv[chan, piece].astype(jnp.float32)
        out_vmem[:, columns] = lax.fori_loop(1, n_chan, add, own_part[AHEAD + piece]).astype(jnp.bfloat16)
        out_move(AHEAD + piece).start()

    @pl.loop(1, n_ctx)
    def _(step):
        peer = lax.rem(me + step, n_ctx)
        out_copy(peer).wait_send()
        back_out(peer).wait_send()

    @pl.loop(1, n_chan)
    def _(step):
        chan = other(step)
        for piece in range(W_PIECES):
            w_move(chan, my_chan, piece).wait_send()
            side_move(chan, quarter, piece).wait_send()
            pair_move(chan, quarter, piece, 0).wait_send()
            pair_move(chan, far_quarter, piece, 1).wait_send()
        for lot in range(lots):
            gated_move(chan, my_chan, lot).wait_send()
        for piece in range(PIECES - AHEAD):
            part_move(chan, my_chan, piece).wait_send()

    for piece in range(PIECES):
        out_move(piece).wait()


def shards(n_ctx, n_chan, query_act, key_act, value_act, filters, skip_scale, w_out):
    block, width = key_act.shape
    feats = w_out.shape[1] // n_chan
    chans = width // n_ctx
    chunk = feats // PIECES
    rest = max(PIECES - AHEAD, 1)
    lots = width // LANES
    forward, inverse = tables(block)
    vmem = pl.BlockSpec(memory_space=pltpu.VMEM)
    dma = pltpu.SemaphoreType.DMA
    return pl.pallas_call(
        functools.partial(kernel, n_ctx, n_chan),
        out_shape=jax.ShapeDtypeStruct((block, feats), jnp.bfloat16),
        in_specs=[pl.BlockSpec(memory_space=pltpu.HBM)] * 8,
        out_specs=pl.BlockSpec(memory_space=pltpu.HBM),
        scratch_shapes=[pltpu.VMEM((block, width), jnp.bfloat16)] * 4 + [
            pltpu.VMEM((1, width), jnp.float32),
            pltpu.VMEM(forward.shape, jnp.bfloat16),
            pltpu.VMEM(inverse.shape, jnp.bfloat16),
            pltpu.VMEM((n_ctx, 2 * chans, block), jnp.bfloat16),
            pltpu.VMEM((n_ctx, 2 * chans, block), jnp.bfloat16),
            pltpu.VMEM((n_ctx, 2 * chans // TILE, TILE, 2 * block), jnp.float32),
            pltpu.VMEM((n_ctx, chans // TILE, TILE, 2 * block), jnp.float32),
            pltpu.VMEM((n_ctx, chans, block), jnp.bfloat16),
            pltpu.VMEM((n_ctx, chans, block), jnp.bfloat16),
            pltpu.VMEM(w_out.shape, jnp.bfloat16),
            pltpu.VMEM((n_chan, width, AHEAD * chunk), jnp.bfloat16),
            pltpu.VMEM((block, width), jnp.bfloat16),
            pltpu.VMEM((n_chan, block, width), jnp.bfloat16),
            pltpu.VMEM((n_chan, rest, block, chunk), jnp.bfloat16),
            pltpu.VMEM((n_chan, rest, block, chunk), jnp.bfloat16),
            pltpu.VMEM((PIECES, block, chunk), jnp.float32),
            dma((n_ctx,)), dma((n_ctx,)), dma((n_ctx,)), dma((n_ctx,)),
            dma((n_chan, rest)), dma((n_chan, rest)), dma((8,)),
            dma((n_chan, W_PIECES)), dma((n_chan, W_PIECES)), dma((n_chan, W_PIECES)), dma((n_chan, W_PIECES)),
            dma((n_chan, 2, W_PIECES)), dma((n_chan, 2, W_PIECES)),
            dma((n_chan, lots)), dma((n_chan, lots)),
            pltpu.VMEM((block, feats), jnp.bfloat16), dma((PIECES,)),
        ],
        compiler_params=pltpu.CompilerParams(
            collective_id=0, has_side_effects=True, vmem_limit_bytes=62 * 1024 * 1024),
    )(query_act, key_act, value_act, filters, skip_scale.reshape(1, width), forward, inverse, w_out)


def solution(mesh):
    return jax.shard_map(
        functools.partial(shards, mesh.shape["ctx"], mesh.shape["chan"]),
        mesh=mesh,
        in_specs=(
            P("ctx", "chan"),
            P("ctx", "chan"),
            P("ctx", "chan"),
            P("ctx", "chan"),
            P("chan"),
            P("chan", None),
        ),
        out_specs=P("ctx", "chan"),
        check_vma=False,
    )
```
